256 devices in a mesh: bin: 4 (over x_hi, core), strip: 64 (over x_lo, z, y).
Axes of the slice: x: 4 (x_hi: 2, x_lo: 2; x = x_hi * 2 + x_lo), y: 4, z: 8, core: 2. Of those that a mesh axis runs over, the one named last changes fastest.
Arguments:
- maps_in: bfloat16 [8, 256, 96, 1024], P('bin', 'strip'), may hold values from -6 to 6
- conv_one: bfloat16 [3, 3, 96, 96], replicated, may hold values from -0.21875 to 0.21875
- conv_two: bfloat16 [3, 3, 96, 96], replicated, may hold values from -0.21875 to 0.21875
- noise_shift: float32 [8, 96], P('bin'), may hold values from -4 to 4
- bin_embed: float32 [8, 96], replicated, may hold values from -3 to 3
- norm_gain: float32 [96], replicated, may hold values from 0.1 to 1.9
- w_query: bfloat16 [96, 96], replicated, may hold values from -0.625 to 0.625
- w_key: bfloat16 [96, 96], replicated, may hold values from -0.625 to 0.625
- w_value: bfloat16 [96, 96], replicated, may hold values from -0.625 to 0.625
- w_out: bfloat16 [96, 96], replicated, may hold values from -0.625 to 0.625
Outputs:
- features: bfloat16 [8, 256, 96, 1024], P('bin', 'strip')
- bottleneck: bfloat16 [8, 128, 96, 512], P('bin', 'strip')
The draws below stay inside these ranges and needn't reach their ends.
All inputs are finite; a program needn't handle non-finite values.
Results may differ from the reference program's by a relative error of at most 0.014.
Values may be sent and summed in bfloat16 or wider, within the bound.
A program may use at most 128 MiB of HBM per device.

```python
import jax
import jax.numpy as jnp
from jax import lax

C = 96
HEADS = 4
HEAD = 24
BINS = 8
COLS = 1024
ROWS = 256


def block_scale(stream_key, extent, pieces, smallest, top_value):
    factor_of, own = 1.0, jax.random.fold_in(stream_key, 6)
    for position, blocks in pieces:
        steps = jnp.exp(jax.random.uniform(jax.random.fold_in(own, position), (blocks,), jnp.float32, smallest / len(pieces), top_value / len(pieces)))
        factor_of = factor_of * jnp.repeat(steps, extent[position] // blocks).reshape([-1 if axis == position else 1 for axis in range(len(extent))])
    return factor_of


def centred(rng, dims, width, most, pieces=(), held_as=jnp.bfloat16):
    array = jax.random.normal(rng, dims, jnp.float32) * width
    if len(pieces) > 0:
        array = block_scale(rng, dims, pieces, -0.22, 0.18) * array
    return jnp.clip(array, min=-most, max=most).astype(held_as)


def setup_inputs(seed: int = 0) -> dict:
    key_of = jax.random.split(jax.random.key(seed), 11)
    return {
        "maps_in": centred(key_of[0], (BINS, ROWS, C, COLS), 1.0, 6.0, ((0, 4), (1, 64))),
        "conv_one": centred(key_of[1], (3, 3, C, C), (9 * C) ** -0.5, 0.21875),
        "conv_two": centred(key_of[2], (3, 3, C, C), (9 * C) ** -0.5, 0.21875),
        "noise_shift": centred(key_of[3], (BINS, C), 1.0, 4.0, ((0, 4),), jnp.float32),
        "bin_embed": centred(key_of[4], (BINS, C), 0.5, 3.0, (), jnp.float32),
        "norm_gain": jnp.clip(1.0 + 0.18 * jax.random.normal(key_of[5], (C,), jnp.float32), 0.1, 1.9),
        "w_query": centred(key_of[6], (C, C), C ** -0.5, 0.625),
        "w_key": centred(key_of[7], (C, C), C ** -0.5, 0.625),
        "w_value": centred(key_of[8], (C, C), C ** -0.5, 0.625),
        "w_out": centred(key_of[9], (C, C), C ** -0.5, 0.625),
    }


def conv_map(plane, kernel):
    rows = plane.shape[0]
    cols = plane.shape[2]
    padded = jnp.pad(plane.astype(jnp.float32), ((1, 1), (0, 0), (1, 1)))
    total = jnp.zeros((rows, kernel.shape[2], cols), jnp.float32)
    for i in range(3):
        for j in range(3):
            total = total + jnp.einsum('oc,rcx->rox', kernel[i, j].astype(jnp.float32), padded[i:i + rows, :, j:j + cols])
    return total

def reference(maps_in, conv_one, conv_two, noise_shift, bin_embed, norm_gain, w_query, w_key, w_value, w_out):
    act = jax.nn.silu(maps_in.astype(jnp.float32)).astype(jnp.bfloat16)
    inner = lax.map(lambda plane: conv_map(plane, conv_one), act) + noise_shift[:, None, :, None]
    second = jax.nn.silu(inner).astype(jnp.bfloat16)
    features = (maps_in.astype(jnp.float32) + lax.map(lambda plane: conv_map(plane, conv_two), second)).astype(jnp.bfloat16)
    full = features.astype(jnp.float32)
    pooled = (0.25 * (full[:, 0::2, :, 0::2] + full[:, 1::2, :, 0::2] + full[:, 0::2, :, 1::2] + full[:, 1::2, :, 1::2])).astype(jnp.bfloat16)
    z_in = pooled.astype(jnp.float32) + bin_embed[:, None, :, None]
    center = lax.optimization_barrier(jnp.mean(z_in, axis=2, keepdims=True))
    spread = lax.optimization_barrier(jnp.mean((z_in - center) ** 2, axis=2, keepdims=True))
    normed = ((z_in - center) * lax.rsqrt(spread + 1e-05) * norm_gain[None, None, :, None]).astype(jnp.bfloat16)
    normed_f = normed.astype(jnp.float32)
    query = jnp.einsum('trcp,cd->trdp', normed_f, w_query.astype(jnp.float32))
    key = jnp.einsum('trcp,cd->trdp', normed_f, w_key.astype(jnp.float32))
    value = jnp.einsum('trcp,cd->trdp', normed_f, w_value.astype(jnp.float32))
    shape5 = (BINS, query.shape[1], HEADS, HEAD, query.shape[3])
    query = query.reshape(shape5)
    key = key.reshape(shape5)
    value = value.reshape(shape5)
    score = jnp.einsum('trhep,urhep->turhp', query, key) / jnp.sqrt(jnp.float32(HEAD))
    expo = jnp.exp(score)
    prob = expo / lax.optimization_barrier(jnp.sum(expo, axis=1, keepdims=True))
    mixed = jnp.einsum('turhp,urhep->trhep', prob, value).reshape(z_in.shape).astype(jnp.bfloat16)
    bottleneck = (z_in + jnp.einsum('trcp,cd->trdp', mixed.astype(jnp.float32), w_out.astype(jnp.float32))).astype(jnp.bfloat16)
    return (features, bottleneck)
```

```python
import jax
import jax.numpy as jnp
from jax import lax
from jax.experimental import pallas as pl
from jax.experimental.pallas import tpu as pltpu
from jax.sharding import PartitionSpec as P

MESH = pl.DeviceIdType.MESH
BF = jnp.bfloat16
F32 = jnp.float32
C = 96
HEADS = 4
HEAD = 24
BINS = 8
X = 1024
PX = 512
TILE = 256


def silu(v):
    half = 0.5 * v
    return half + half * jnp.tanh(half)


def column(row, width):
    eye = lax.broadcasted_iota(jnp.int32, (C, C), 0) == lax.broadcasted_iota(jnp.int32, (C, C), 1)
    col = jnp.sum(jnp.where(eye, jnp.broadcast_to(row, (C, C)), 0.0), axis=1, keepdims=True)
    return jnp.broadcast_to(col, (C, width))


def kernel(
    x_ref, conv_one, conv_two, noise, embed, gain, w_query, w_key, w_value, w_out,
    f_ref, o_ref,
    xin, k1, k2, b1, b2, feat, shift, ecol, gcol, wqkv, wout, table,
    pooled, tokens, qkv, mixed, result,
    load_sem, halo_send, halo_recv, feat_sem, pool_send, pool_recv, back_send, back_recv,
):
    strip = lax.axis_index("strip")
    bdev = lax.axis_index("bin")
    core = lax.rem(bdev, 2)
    xh = bdev // 2
    other = (1 - xh) * 2
    sibling = xh * 2 + 1 - core
    last = lax.axis_size("strip") - 1
    has_up = strip > 0
    has_dn = strip < last
    up = jnp.maximum(strip - 1, 0)
    dn = jnp.minimum(strip + 1, last)

    loads = [
        pltpu.make_async_copy(x_ref.at[b], xin.at[b, pl.ds(2, 4)], load_sem.at[b]) for b in range(2)
    ]
    for copy in loads:
        copy.start()

    barrier = pltpu.get_barrier_semaphore()
    for device in ({"bin": other}, {"bin": other + 1}, {"bin": sibling}):
        pl.semaphore_signal(barrier, inc=1, device_id=device, device_id_type=MESH)

    @pl.when(has_up)
    def _():
        pl.semaphore_signal(barrier, inc=1, device_id={"strip": up}, device_id_type=MESH)

    @pl.when(has_dn)
    def _():
        pl.semaphore_signal(barrier, inc=1, device_id={"strip": dn}, device_id_type=MESH)

    pl.semaphore_wait(barrier, 3 + has_up.astype(jnp.int32) + has_dn.astype(jnp.int32))

    def to_down(b):
        return pltpu.make_async_remote_copy(
            x_ref.at[b, pl.ds(2, 2)], xin.at[b, pl.ds(0, 2)], halo_send.at[b, 0], halo_recv.at[b, 0],
            device_id={"strip": dn}, device_id_type=MESH,
        )

    def to_up(b):
        return pltpu.make_async_remote_copy(
            x_ref.at[b, pl.ds(0, 2)], xin.at[b, pl.ds(6, 2)], halo_send.at[b, 1], halo_recv.at[b, 1],
            device_id={"strip": up}, device_id_type=MESH,
        )

    for b in range(2):

        @pl.when(has_dn)
        def _():
            to_down(b).start()

        @pl.when(has_up)
        def _():
            to_up(b).start()

    for conv, packed in ((conv_one, k1), (conv_two, k2)):
        packed[...] = jnp.zeros_like(packed)
        flat = jnp.concatenate([conv[i, j] for i in range(3) for j in range(3)], axis=1)
        packed[pl.ds(0, C), pl.ds(0, 9 * C)] = flat
        packed[pl.ds(C, C), :] = jnp.concatenate([jnp.zeros((C, 3 * C), BF), flat], axis=1)
    for b in range(2):
        both = column(noise[pl.ds(b, 1), :], TILE)
        shift[b, pl.ds(0, C), :] = both
        shift[b, pl.ds(C, C), :] = both
    for t in range(BINS):
        ecol[t] = column(embed[pl.ds(t, 1), :], 128)
    gcol[...] = column(gain[...], 128)
    row = lax.broadcasted_iota(jnp.int32, (C, C), 0)
    col = lax.broadcasted_iota(jnp.int32, (C, C), 1)
    perm = jnp.where(col == lax.rem(row, HEADS) * HEAD + row // HEADS, 1.0, 0.0).astype(BF)
    eye = jnp.where(row == col, 1.0, 0.0).astype(BF)
    for index, weight in enumerate((w_key, w_value, w_query)):
        moved = lax.dot_general(
            perm, weight[...], (((1,), (1,)), ((), ())), preferred_element_type=F32
        )
        wqkv[pl.ds(index * C, C), :] = moved.astype(BF)
    moved = jnp.dot(perm, w_out[...], preferred_element_type=F32).astype(BF)
    wout[...] = lax.dot_general(
        eye, moved, (((1,), (1,)), ((), ())), preferred_element_type=F32
    ).astype(BF)
    source = lax.broadcasted_iota(jnp.int32, (TILE, TILE // 2), 0)
    target = lax.broadcasted_iota(jnp.int32, (TILE, TILE // 2), 1)
    table[...] = jnp.where(source // 2 == target, 0.25, 0.0).astype(BF)

    lane = lax.broadcasted_iota(jnp.int32, (32, X), 1)
    first_lane = lane == 0
    final_lane = lane == X - 1

    def spread(ref, b, at, value):
        ref[b, pl.ds(at, 32), :] = jnp.where(first_lane, 0.0, pltpu.roll(value, 1, 1)).astype(BF)
        ref[b, pl.ds(at + 2 * C, 32), :] = jnp.where(
            final_lane, 0.0, pltpu.roll(value, X - 1, 1)
        ).astype(BF)

    def activate(b, q0, count):
        def body(step, carry):
            q, block = q0 + step // 3, lax.rem(step, 3) * 32
            value = silu(xin[b, q, pl.ds(pl.multiple_of(block, 32), 32), :].astype(F32))
            at = pl.multiple_of(q * 288 + block, 32)
            b1[b, pl.ds(at + C, 32), :] = value.astype(BF)
            spread(b1, b, at, value)
            return carry

        lax.fori_loop(0, 3 * count, body, 0)

    def first_conv(b, pair):
        def body(n, carry):
            cols = pl.ds(pl.multiple_of(n * TILE, TILE), TILE)
            start = pl.multiple_of(pair * 576, 64)
            total = jnp.dot(
                k1[...], b1[b, pl.ds(start, 1152), cols], preferred_element_type=F32
            )
            value = silu(total + shift[b])
            off_top = jnp.logical_and(pair == 0, jnp.logical_not(has_up))
            off_end = jnp.logical_and(pair == 2, jnp.logical_not(has_dn))
            upper = jnp.where(off_top, 0.0, value[:C]).astype(BF)
            lower = jnp.where(off_end, 0.0, value[C:]).astype(BF)
            b2[b, pl.ds(pl.multiple_of(start + C, 32), C), cols] = upper
            b2[b, pl.ds(pl.multiple_of(start + 288 + C, 32), C), cols] = lower
            return carry

        lax.fori_loop(0, X // TILE, body, 0)

        def sides(step, carry):
            at = pl.multiple_of(pair * 576 + (step // 3) * 288 + lax.rem(step, 3) * 32, 32)
            spread(b2, b, at, b2[b, pl.ds(at + C, 32), :].astype(F32))
            return carry

        lax.fori_loop(0, 6, sides, 0)

    def second_conv(b, half):
        def body(n, carry):
            cols = pl.ds(pl.multiple_of(n * TILE, TILE), TILE)
            start = pl.multiple_of(half * 576, 64)
            total = jnp.dot(
                k2[...], b2[b, pl.ds(start, 1152), cols], preferred_element_type=F32
            )
            value = [
                (xin[b, 2 + 2 * half + r, :, cols].astype(F32) + total[r * C : (r + 1) * C]).astype(BF)
                for r in range(2)
            ]
            for r in range(2):
                feat[b, 2 * half + r, :, cols] = value[r]
            mean = jnp.dot(value[0], table[...], preferred_element_type=F32) + jnp.dot(
                value[1], table[...], preferred_element_type=F32
            )
            px = pl.ds(pl.multiple_of(n * (TILE // 2), TILE // 2), TILE // 2)
            pooled[b, half, :, px] = mean.astype(BF)
            return carry

        lax.fori_loop(0, X // TILE, body, 0)

    for b in range(2):
        loads[b].wait()
        activate(b, 2, 4)
        first_conv(b, 1)

    def feature_out(b, half):
        rows = pl.ds(2 * half, 2)
        return pltpu.make_async_copy(feat.at[b, rows], f_ref.at[b, rows], feat_sem.at[b, half])

    def pool_far(b, half):
        return pltpu.make_async_remote_copy(
            pooled.at[b, half], tokens.at[2 * bdev + b], pool_send.at[b, half, 0],
            pool_recv.at[2 * bdev + b], device_id={"bin": other + half}, device_id_type=MESH,
        )

    def pool_near(b, half):
        return pltpu.make_async_remote_copy(
            pooled.at[b, half], tokens.at[2 * bdev + b], pool_send.at[b, half, 1],
            pool_recv.at[2 * bdev + b], device_id={"bin": sibling}, device_id_type=MESH,
        )

    def pool_here(b, half):
        return pltpu.make_async_copy(
            pooled.at[b, half], tokens.at[2 * bdev + b], pool_recv.at[2 * bdev + b]
        )

    def unit(step, carry):
        b, half = step // 2, lax.rem(step, 2)

        @pl.when(half == 0)
        def _():
            @pl.when(has_up)
            def _():
                to_down(b).wait_recv()

            @pl.when(jnp.logical_not(has_up))
            def _():
                xin[b, pl.ds(0, 2)] = jnp.zeros((2, C, X), BF)

        @pl.when(half == 1)
        def _():
            @pl.when(has_dn)
            def _():
                to_up(b).wait_recv()

            @pl.when(jnp.logical_not(has_dn))
            def _():
                xin[b, pl.ds(6, 2)] = jnp.zeros((2, C, X), BF)

        activate(b, 6 * half, 2)
        first_conv(b, 2 * half)
        second_conv(b, half)
        pool_far(b, half).start()

        @pl.when(half == core)
        def _():
            pool_here(b, half).start()

        @pl.when(half != core)
        def _():
            pool_near(b, half).start()

        feature_out(b, half).start()
        return carry

    lax.fori_loop(0, 4, unit, 0)

    def token(t):
        return [
            tokens[t, :, pl.ds(n * 128, 128)].astype(F32) + ecol[t] for n in range(PX // 128)
        ]

    def project(step, carry):
        t = lax.rem(2 * bdev + step, BINS)
        pltpu.make_async_copy(tokens.at[t], tokens.at[t], pool_recv.at[t]).wait()
        normed = []
        for z in token(t):
            center = jnp.sum(z, axis=0, keepdims=True) * (1.0 / C)
            delta = z - center
            spread_of = jnp.sum(delta * delta, axis=0, keepdims=True) * (1.0 / C)
            normed.append((delta * lax.rsqrt(spread_of + 1e-05) * gcol[...]).astype(BF))
        qkv[t] = jnp.dot(
            wqkv[...], jnp.concatenate(normed, axis=1), preferred_element_type=F32
        )
        return carry

    lax.fori_loop(0, BINS, project, 0)

    scale = 1.0 / (HEAD**0.5)

    def attend(step, carry):
        index, n = step // 4, lax.rem(step, 4)
        t = xh * 4 + index
        px = pl.ds(pl.multiple_of(n * 128, 128), 128)
        query = (qkv[t, pl.ds(2 * C, C), px] * scale).reshape(12, 8, 128)
        numer = jnp.zeros((12, 8, 128), F32)
        denom = jnp.zeros((8, 128), F32)
        for u in range(BINS):
            score = jnp.sum(query * qkv[u, pl.ds(0, C), px].reshape(12, 8, 128), axis=0)
            expo = jnp.exp(score + pltpu.roll(score, 4, 0))
            denom = denom + expo
            numer = numer + qkv[u, pl.ds(C, C), px].reshape(12, 8, 128) * expo[None]
        mixed[index, :, px] = (numer / denom[None]).reshape(C, 128).astype(BF)
        return carry

    lax.fori_loop(0, 16, attend, 0)

    def finish(index, carry):
        t = xh * 4 + index
        delta = jnp.dot(wout[...], mixed[index], preferred_element_type=F32)
        result[index] = (jnp.concatenate(token(t), axis=1) + delta).astype(BF)
        return carry

    lax.fori_loop(0, 4, finish, 0)

    def back(b):
        return pltpu.make_async_remote_copy(
            result.at[2 * (1 - core) + b], o_ref.at[b, core], back_send.at[b], back_recv.at[b],
            device_id={"bin": sibling}, device_id_type=MESH,
        )

    def keep(b):
        return pltpu.make_async_copy(result.at[2 * core + b], o_ref.at[b, core], load_sem.at[b])

    for b in range(2):
        back(b).start()
    for b in range(2):
        keep(b).start()

    def drain(step, carry):
        b, half = step // 2, lax.rem(step, 2)
        feature_out(b, half).wait()
        pool_far(b, half).wait_send()

        @pl.when(half != core)
        def _():
            pool_near(b, half).wait_send()

        return carry

    lax.fori_loop(0, 4, drain, 0)
    for b in range(2):

        @pl.when(has_dn)
        def _():
            to_down(b).wait_send()

        @pl.when(has_up)
        def _():
            to_up(b).wait_send()

        back(b).wait()
        keep(b).wait()


def local(
    maps_in, conv_one, conv_two, noise_shift, bin_embed, norm_gain, w_query, w_key, w_value, w_out
):
    whole = pl.BlockSpec(memory_space=pltpu.VMEM)
    hbm = pl.BlockSpec(memory_space=pl.ANY)
    return pl.pallas_call(
        kernel,
        out_shape=(
            jax.ShapeDtypeStruct((2, 4, C, X), BF),
            jax.ShapeDtypeStruct((2, 2, C, PX), BF),
        ),
        in_specs=[hbm] + [whole] * 9,
        out_specs=(hbm, hbm),
        scratch_shapes=[
            pltpu.VMEM((2, 8, C, X), BF),
            pltpu.VMEM((2 * C, 12 * C), BF),
            pltpu.VMEM((2 * C, 12 * C), BF),
            pltpu.VMEM((2, 24 * C, X), BF),
            pltpu.VMEM((2, 18 * C, X), BF),
            pltpu.VMEM((2, 4, C, X), BF),
            pltpu.VMEM((2, 2 * C, TILE), F32),
            pltpu.VMEM((BINS, C, 128), F32),
            pltpu.VMEM((C, 128), F32),
            pltpu.VMEM((3 * C, C), BF),
            pltpu.VMEM((C, C), BF),
            pltpu.VMEM((TILE, TILE // 2), BF),
            pltpu.VMEM((2, 2, C, PX), BF),
            pltpu.VMEM((BINS, C, PX), BF),
            pltpu.VMEM((BINS, 3 * C, PX), F32),
            pltpu.VMEM((4, C, PX), BF),
            pltpu.VMEM((4, C, PX), BF),
            pltpu.SemaphoreType.DMA((2,)),
            pltpu.SemaphoreType.DMA((2, 2)),
            pltpu.SemaphoreType.DMA((2, 2)),
            pltpu.SemaphoreType.DMA((2, 2)),
            pltpu.SemaphoreType.DMA((2, 2, 2)),
            pltpu.SemaphoreType.DMA((BINS,)),
            pltpu.SemaphoreType.DMA((2,)),
            pltpu.SemaphoreType.DMA((2,)),
        ],
        compiler_params=pltpu.CompilerParams(
            collective_id=0, has_side_effects=True, vmem_limit_bytes=60 * 1024 * 1024
        ),
        name="resblock_attention",
    )(
        maps_in, conv_one, conv_two, noise_shift, bin_embed, norm_gain.reshape(1, C),
        w_query, w_key, w_value, w_out,
    )


def solution(mesh):
    in_specs = (
        P("bin", "strip", None, None),
        P(),
        P(),
        P("bin", None),
        P(),
        P(),
        P(),
        P(),
        P(),
        P(),
    )
    out_specs = (P("bin", "strip", None, None), P("bin", "strip", None, None))
    return jax.shard_map(local, mesh=mesh, in_specs=in_specs, out_specs=out_specs, check_vma=False)
```

```python
import jax
import jax.numpy as jnp
from jax import lax
from jax.experimental import pallas as pl
from jax.experimental.pallas import tpu as pltpu
from jax.sharding import PartitionSpec as P

MESH = pl.DeviceIdType.MESH
BF = jnp.bfloat16
F32 = jnp.float32
C = 96
HEADS = 4
HEAD = 24
BINS = 8
X = 1024
PX = 512
TILE = 256

ALL = dict(act=(0, 1024, 0), one=(0, 4), side=(0, 1024, 0), two=(0, 4))
FRONT = dict(act=(0, 640, 0), one=(0, 2), side=(0, 512, 0), two=(0, 1))
REST = dict(act=(384, 1024, 512), one=(2, 4), side=(256, 1024, 384), two=(1, 4))
PIECES = ((0, 640), (640, 384))


def silu(v):
    half = 0.5 * v
    return half + half * jnp.tanh(half)


def column(row, width):
    eye = lax.broadcasted_iota(jnp.int32, (C, C), 0) == lax.broadcasted_iota(jnp.int32, (C, C), 1)
    col = jnp.sum(jnp.where(eye, jnp.broadcast_to(row, (C, C)), 0.0), axis=1, keepdims=True)
    return jnp.broadcast_to(col, (C, width))


def kernel(
    x_ref, conv_one, conv_two, noise, embed, gain, w_query, w_key, w_value, w_out,
    f_ref, o_ref,
    xin, k1, k2, b1, b2, feat, shift, ecol, gcol, wqkv, wout, table,
    pooled, tokens, qkv, mixed, result,
    load_sem, halo_send, halo_recv, feat_sem, pool_send, pool_recv, back_send, back_recv,
):
    strip = lax.axis_index("strip")
    bdev = lax.axis_index("bin")
    core = lax.rem(bdev, 2)
    xh = bdev // 2
    other = (1 - xh) * 2
    sibling = xh * 2 + 1 - core
    last = lax.axis_size("strip") - 1
    has_up = strip > 0
    has_dn = strip < last
    up = jnp.maximum(strip - 1, 0)
    dn = jnp.minimum(strip + 1, last)

    loads = [
        pltpu.make_async_copy(x_ref.at[b], xin.at[b, pl.ds(2, 4)], load_sem.at[b]) for b in range(2)
    ]
    for copy in loads:
        copy.start()

    barrier = pltpu.get_barrier_semaphore()
    for device in ({"bin": other}, {"bin": other + 1}, {"bin": sibling}):
        pl.semaphore_signal(barrier, inc=1, device_id=device, device_id_type=MESH)

    @pl.when(has_up)
    def _():
        pl.semaphore_signal(barrier, inc=1, device_id={"strip": up}, device_id_type=MESH)

    @pl.when(has_dn)
    def _():
        pl.semaphore_signal(barrier, inc=1, device_id={"strip": dn}, device_id_type=MESH)

    pl.semaphore_wait(barrier, 3 + has_up.astype(jnp.int32) + has_dn.astype(jnp.int32))

    def to_down(b, piece):
        cols = pl.ds(*PIECES[piece])
        return pltpu.make_async_remote_copy(
            x_ref.at[b, pl.ds(2, 2), :, cols], xin.at[b, pl.ds(0, 2), :, cols],
            halo_send.at[b, 0, piece], halo_recv.at[b, 0, piece],
            device_id={"strip": dn}, device_id_type=MESH,
        )

    def to_up(b, piece):
        cols = pl.ds(*PIECES[piece])
        return pltpu.make_async_remote_copy(
            x_ref.at[b, pl.ds(0, 2), :, cols], xin.at[b, pl.ds(6, 2), :, cols],
            halo_send.at[b, 1, piece], halo_recv.at[b, 1, piece],
            device_id={"strip": up}, device_id_type=MESH,
        )

    for b in range(2):
        for piece in range(2):

            @pl.when(has_dn)
            def _():
                to_down(b, piece).start()

            @pl.when(has_up)
            def _():
                to_up(b, piece).start()

    for conv, packed in ((conv_one, k1), (conv_two, k2)):
        packed[...] = jnp.zeros_like(packed)
        flat = jnp.concatenate([conv[i, j] for i in range(3) for j in range(3)], axis=1)
        packed[pl.ds(0, C), pl.ds(0, 9 * C)] = flat
        packed[pl.ds(C, C), :] = jnp.concatenate([jnp.zeros((C, 3 * C), BF), flat], axis=1)
    for b in range(2):
        both = column(noise[pl.ds(b, 1), :], TILE)
        shift[b, pl.ds(0, C), :] = both
        shift[b, pl.ds(C, C), :] = both
    for t in range(BINS):
        ecol[t] = column(embed[pl.ds(t, 1), :], 128)
    gcol[...] = column(gain[...], 128)
    row = lax.broadcasted_iota(jnp.int32, (C, C), 0)
    col = lax.broadcasted_iota(jnp.int32, (C, C), 1)
    perm = jnp.where(col == lax.rem(row, HEADS) * HEAD + row // HEADS, 1.0, 0.0).astype(BF)
    eye = jnp.where(row == col, 1.0, 0.0).astype(BF)
    for index, weight in enumerate((w_key, w_value, w_query)):
        moved = lax.dot_general(
            perm, weight[...], (((1,), (1,)), ((), ())), preferred_element_type=F32
        )
        wqkv[pl.ds(index * C, C), :] = moved.astype(BF)
    moved = jnp.dot(perm, w_out[...], preferred_element_type=F32).astype(BF)
    wout[...] = lax.dot_general(
        eye, moved, (((1,), (1,)), ((), ())), preferred_element_type=F32
    ).astype(BF)
    source = lax.broadcasted_iota(jnp.int32, (TILE, TILE // 2), 0)
    target = lax.broadcasted_iota(jnp.int32, (TILE, TILE // 2), 1)
    table[...] = jnp.where(source // 2 == target, 0.25, 0.0).astype(BF)

    def spread(ref, b, at, value, lo, keep_from):
        width = value.shape[1]
        lane = lax.broadcasted_iota(jnp.int32, (32, width), 1)
        left, right = pltpu.roll(value, 1, 1), pltpu.roll(value, width - 1, 1)
        if lo == 0:
            left = jnp.where(lane == 0, jnp.zeros_like(left), left)
        if lo + width == X:
            right = jnp.where(lane == width - 1, jnp.zeros_like(right), right)
        cols = pl.ds(keep_from, lo + width - keep_from)
        ref[b, pl.ds(at, 32), cols] = left[:, keep_from - lo :]
        ref[b, pl.ds(at + 2 * C, 32), cols] = right[:, keep_from - lo :]

    def activate(b, q0, count, phase=ALL):
        lo, hi, keep_from = phase["act"]

        def body(step, carry):
            q, block = q0 + step // 3, lax.rem(step, 3) * 32
            value = silu(
                xin[b, q, pl.ds(pl.multiple_of(block, 32), 32), pl.ds(lo, hi - lo)].astype(F32)
            ).astype(BF)
            at = pl.multiple_of(q * 288 + block, 32)
            b1[b, pl.ds(at + C, 32), pl.ds(keep_from, hi - keep_from)] = (
                value[:, keep_from - lo :]
            )
            spread(b1, b, at, value, lo, keep_from)
            return carry

        lax.fori_loop(0, 3 * count, body, 0, unroll=3)

    def first_conv(b, pair, phase=ALL):
        lo, hi, keep_from = phase["side"]

        def body(n, carry):
            cols = pl.ds(pl.multiple_of(n * TILE, TILE), TILE)
            start = pl.multiple_of(pair * 576, 64)
            total = jnp.dot(
                k1[...], b1[b, pl.ds(start, 1152), cols], preferred_element_type=F32
            )
            value = silu(total + shift[b])
            off_top = jnp.logical_and(pair == 0, jnp.logical_not(has_up))
            off_end = jnp.logical_and(pair == 2, jnp.logical_not(has_dn))
            upper = jnp.where(off_top, 0.0, value[:C]).astype(BF)
            lower = jnp.where(off_end, 0.0, value[C:]).astype(BF)
            b2[b, pl.ds(pl.multiple_of(start + C, 32), C), cols] = upper
            b2[b, pl.ds(pl.multiple_of(start + 288 + C, 32), C), cols] = lower
            return carry

        lax.fori_loop(*phase["one"], body, 0, unroll=True)

        def sides(step, carry):
            at = pl.multiple_of(pair * 576 + (step // 3) * 288 + lax.rem(step, 3) * 32, 32)
            value = b2[b, pl.ds(at + C, 32), pl.ds(lo, hi - lo)]
            spread(b2, b, at, value, lo, keep_from)
            return carry

        lax.fori_loop(0, 6, sides, 0, unroll=3)

    def second_conv(b, half, phase=ALL):
        def body(n, carry):
            cols = pl.ds(pl.multiple_of(n * TILE, TILE), TILE)
            start = pl.multiple_of(half * 576, 64)
            total = jnp.dot(
                k2[...], b2[b, pl.ds(start, 1152), cols], preferred_element_type=F32
            )
            value = [
                (xin[b, 2 + 2 * half + r, :, cols].astype(F32) + total[r * C : (r + 1) * C]).astype(BF)
                for r in range(2)
            ]
            for r in range(2):
                feat[b, 2 * half + r, :, cols] = value[r]
            mean = jnp.dot(value[0], table[...], preferred_element_type=F32) + jnp.dot(
                value[1], table[...], preferred_element_type=F32
            )
            px = pl.ds(pl.multiple_of(n * (TILE // 2), TILE // 2), TILE // 2)
            pooled[b, half, :, px] = mean.astype(BF)
            pool_far(b, half, px).start()

            @pl.when(half == core)
            def _():
                pool_here(b, half, px).start()

            @pl.when(half != core)
            def _():
                pool_near(b, half, px).start()

            return carry

        lax.fori_loop(*phase["two"], body, 0, unroll=True)

    for b in range(2):
        loads[b].wait()
        activate(b, 2, 4)
        first_conv(b, 1)

    def feature_out(b, half):
        rows = pl.ds(2 * half, 2)
        return pltpu.make_async_copy(feat.at[b, rows], f_ref.at[b, rows], feat_sem.at[b, half])

    def pool_far(b, half, px):
        return pltpu.make_async_remote_copy(
            pooled.at[b, half, :, px], tokens.at[2 * bdev + b, :, px], pool_send.at[b, half, 0],
            pool_recv.at[2 * bdev + b], device_id={"bin": other + half}, device_id_type=MESH,
        )

    def pool_near(b, half, px):
        return pltpu.make_async_remote_copy(
            pooled.at[b, half, :, px], tokens.at[2 * bdev + b, :, px], pool_send.at[b, half, 1],
            pool_recv.at[2 * bdev + b], device_id={"bin": sibling}, device_id_type=MESH,
        )

    def pool_here(b, half, px):
        return pltpu.make_async_copy(
            pooled.at[b, half, :, px], tokens.at[2 * bdev + b, :, px], pool_recv.at[2 * bdev + b]
        )

    whole = pl.ds(0, PX)

    def halo(b, half, pieces):
        @pl.when(half == 0)
        def _():
            for piece in pieces:
                cols = pl.ds(*PIECES[piece])

                @pl.when(has_up)
                def _():
                    to_down(b, piece).wait_recv()

                @pl.when(jnp.logical_not(has_up))
                def _():
                    xin[b, pl.ds(0, 2), :, cols] = jnp.zeros((2, C, PIECES[piece][1]), BF)

        @pl.when(half == 1)
        def _():
            for piece in pieces:
                cols = pl.ds(*PIECES[piece])

                @pl.when(has_dn)
                def _():
                    to_up(b, piece).wait_recv()

                @pl.when(jnp.logical_not(has_dn))
                def _():
                    xin[b, pl.ds(6, 2), :, cols] = jnp.zeros((2, C, PIECES[piece][1]), BF)

    flip = jnp.where(lax.rem(strip, 4) == 0, 1, 0)

    def units(b, pieces, phase, final):
        def unit(step, carry):
            half = lax.rem(step + flip, 2)
            halo(b, half, pieces)
            activate(b, 6 * half, 2, phase)
            first_conv(b, 2 * half, phase)
            second_conv(b, half, phase)
            if final:
                feature_out(b, half).start()
            return carry

        lax.fori_loop(0, 2, unit, 0)

    units(0, (0, 1), ALL, True)
    units(1, (0, 1), ALL, True)

    def token(t):
        return [
            tokens[t, :, pl.ds(n * 128, 128)].astype(F32) + ecol[t] for n in range(PX // 128)
        ]

    def project(step, carry):
        step_dev = lax.rem(step, 4)
        peer = 2 * lax.rem(xh + step_dev // 2, 2) + lax.rem(core + step_dev, 2)
        t = 2 * peer + step // 4
        pltpu.make_async_copy(tokens.at[t], tokens.at[t], pool_recv.at[t]).wait()
        normed = []
        for z in token(t):
            center = jnp.sum(z, axis=0, keepdims=True) * (1.0 / C)
            delta = z - center
            spread_of = jnp.sum(delta * delta, axis=0, keepdims=True) * (1.0 / C)
            normed.append((delta * lax.rsqrt(spread_of + 1e-05) * gcol[...]).astype(BF))
        qkv[t] = jnp.dot(
            wqkv[...], jnp.concatenate(normed, axis=1), preferred_element_type=F32
        )
        return carry

    lax.fori_loop(0, BINS, project, 0, unroll=2)

    scale = 1.0 / (HEAD**0.5)

    def back(b, px):
        return pltpu.make_async_remote_copy(
            result.at[2 * (1 - core) + b, :, px], o_ref.at[b, core, :, px], back_send.at[b],
            back_recv.at[b], device_id={"bin": sibling}, device_id_type=MESH,
        )

    def keep(b, px):
        return pltpu.make_async_copy(
            result.at[2 * core + b, :, px], o_ref.at[b, core, :, px], load_sem.at[b]
        )

    def attend(n, carry):
        px = pl.ds(pl.multiple_of(n * 128, 128), 128)

        def one(index, carry):
            t = xh * 4 + index
            query = (qkv[t, pl.ds(2 * C, C), px] * scale).reshape(12, 8, 128)
            numer = jnp.zeros((12, 8, 128), F32)
            denom = jnp.zeros((8, 128), F32)
            for u in range(BINS):
                score = jnp.sum(query * qkv[u, pl.ds(0, C), px].reshape(12, 8, 128), axis=0)
                expo = jnp.exp(score + pltpu.roll(score, 4, 0))
                denom = denom + expo
                numer = numer + qkv[u, pl.ds(C, C), px].reshape(12, 8, 128) * expo[None]
            mixed[:, pl.ds(pl.multiple_of(index * 128, 128), 128)] = (
                (numer / denom[None]).reshape(C, 128).astype(BF)
            )
            return carry

        lax.fori_loop(0, 4, one, 0, unroll=2)
        delta = jnp.dot(wout[...], mixed[...], preferred_element_type=F32)
        for index in range(4):
            t = xh * 4 + index
            result[index, :, px] = (
                tokens[t, :, px].astype(F32) + ecol[t] + delta[:, index * 128 : (index + 1) * 128]
            ).astype(BF)
        for b in range(2):
            back(b, px).start()
            keep(b, px).start()
        return carry

    lax.fori_loop(0, PX // 128, attend, 0)

    def drain(step, carry):
        b, half = step // 2, lax.rem(step, 2)
        feature_out(b, half).wait()
        pool_far(b, half, whole).wait_send()

        @pl.when(half != core)
        def _():
            pool_near(b, half, whole).wait_send()

        return carry

    lax.fori_loop(0, 4, drain, 0)
    for b in range(2):

        for piece in range(2):

            @pl.when(has_dn)
            def _():
                to_down(b, piece).wait_send()

            @pl.when(has_up)
            def _():
                to_up(b, piece).wait_send()

        back(b, whole).wait()
        keep(b, whole).wait()


def local(
    maps_in, conv_one, conv_two, noise_shift, bin_embed, norm_gain, w_query, w_key, w_value, w_out
):
    whole = pl.BlockSpec(memory_space=pltpu.VMEM)
    hbm = pl.BlockSpec(memory_space=pl.ANY)
    return pl.pallas_call(
        kernel,
        out_shape=(
            jax.ShapeDtypeStruct((2, 4, C, X), BF),
            jax.ShapeDtypeStruct((2, 2, C, PX), BF),
        ),
        in_specs=[hbm] + [whole] * 9,
        out_specs=(hbm, hbm),
        scratch_shapes=[
            pltpu.VMEM((2, 8, C, X), BF),
            pltpu.VMEM((2 * C, 12 * C), BF),
            pltpu.VMEM((2 * C, 12 * C), BF),
            pltpu.VMEM((2, 24 * C, X), BF),
            pltpu.VMEM((2, 18 * C, X), BF),
            pltpu.VMEM((2, 4, C, X), BF),
            pltpu.VMEM((2, 2 * C, TILE), F32),
            pltpu.VMEM((BINS, C, 128), F32),
            pltpu.VMEM((C, 128), F32),
            pltpu.VMEM((3 * C, C), BF),
            pltpu.VMEM((C, C), BF),
            pltpu.VMEM((TILE, TILE // 2), BF),
            pltpu.VMEM((2, 2, C, PX), BF),
            pltpu.VMEM((BINS, C, PX), BF),
            pltpu.VMEM((BINS, 3 * C, PX), F32),
            pltpu.VMEM((C, PX), BF),
            pltpu.VMEM((4, C, PX), BF),
            pltpu.SemaphoreType.DMA((2,)),
            pltpu.SemaphoreType.DMA((2, 2, 2)),
            pltpu.SemaphoreType.DMA((2, 2, 2)),
            pltpu.SemaphoreType.DMA((2, 2)),
            pltpu.SemaphoreType.DMA((2, 2, 2)),
            pltpu.SemaphoreType.DMA((BINS,)),
            pltpu.SemaphoreType.DMA((2,)),
            pltpu.SemaphoreType.DMA((2,)),
        ],
        compiler_params=pltpu.CompilerParams(
            collective_id=0, has_side_effects=True, vmem_limit_bytes=60 * 1024 * 1024
        ),
        name="resblock_attention",
    )(
        maps_in, conv_one, conv_two, noise_shift, bin_embed, norm_gain.reshape(1, C),
        w_query, w_key, w_value, w_out,
    )


def solution(mesh):
    in_specs = (
        P("bin", "strip", None, None),
        P(),
        P(),
        P("bin", None),
        P(),
        P(),
        P(),
        P(),
        P(),
        P(),
    )
    out_specs = (P("bin", "strip", None, None), P("bin", "strip", None, None))
    return jax.shard_map(local, mesh=mesh, in_specs=in_specs, out_specs=out_specs, check_vma=False)
```

```python
import jax
import jax.numpy as jnp
from jax import lax
from jax.experimental import pallas as pl
from jax.experimental.pallas import tpu as pltpu
from jax.sharding import PartitionSpec as P

MESH = pl.DeviceIdType.MESH
BF = jnp.bfloat16
F32 = jnp.float32
C = 96
HEADS = 4
HEAD = 24
BINS = 8
X = 1024
PX = 512
TILE = 512

ALL = dict(act=(0, 1024, 0), one=(0, 2), side=(0, 1024, 0), two=(0, 2))
PIECES = ((0, 1024),)


def silu(v):
    half = 0.5 * v
    return half + half * jnp.tanh(half)


def column(row, width):
    eye = lax.broadcasted_iota(jnp.int32, (C, C), 0) == lax.broadcasted_iota(jnp.int32, (C, C), 1)
    col = jnp.sum(jnp.where(eye, jnp.broadcast_to(row, (C, C)), 0.0), axis=1, keepdims=True)
    return jnp.broadcast_to(col, (C, width))


def kernel(
    x_ref, conv_one, conv_two, noise, embed, gain, w_query, w_key, w_value, w_out,
    f_ref, o_ref,
    xin, k1, k2, b1, b2, feat, shift, ecol, gcol, wqkv, wout, table,
    pooled, tokens, qkv, mixed, result,
    load_sem, halo_send, halo_recv, feat_sem, pool_send, pool_recv, back_send, back_recv,
):
    strip = lax.axis_index("strip")
    bdev = lax.axis_index("bin")
    core = lax.rem(bdev, 2)
    xh = bdev // 2
    other = (1 - xh) * 2
    sibling = xh * 2 + 1 - core
    last = lax.axis_size("strip") - 1
    has_up = strip > 0
    has_dn = strip < last
    up = jnp.maximum(strip - 1, 0)
    dn = jnp.minimum(strip + 1, last)

    loads = [
        pltpu.make_async_copy(x_ref.at[b], xin.at[b, pl.ds(2, 4)], load_sem.at[b]) for b in range(2)
    ]
    for copy in loads:
        copy.start()

    barrier = pltpu.get_barrier_semaphore()
    for device in ({"bin": other}, {"bin": other + 1}, {"bin": sibling}):
        pl.semaphore_signal(barrier, inc=1, device_id=device, device_id_type=MESH)

    @pl.when(has_up)
    def _():
        pl.semaphore_signal(barrier, inc=1, device_id={"strip": up}, device_id_type=MESH)

    @pl.when(has_dn)
    def _():
        pl.semaphore_signal(barrier, inc=1, device_id={"strip": dn}, device_id_type=MESH)

    pl.semaphore_wait(barrier, 3 + has_up.astype(jnp.int32) + has_dn.astype(jnp.int32))

    def to_down(b, piece):
        cols = pl.ds(*PIECES[piece])
        return pltpu.make_async_remote_copy(
            x_ref.at[b, pl.ds(2, 2), :, cols], xin.at[b, pl.ds(0, 2), :, cols],
            halo_send.at[b, 0, piece], halo_recv.at[b, 0, piece],
            device_id={"strip": dn}, device_id_type=MESH,
        )

    def to_up(b, piece):
        cols = pl.ds(*PIECES[piece])
        return pltpu.make_async_remote_copy(
            x_ref.at[b, pl.ds(0, 2), :, cols], xin.at[b, pl.ds(6, 2), :, cols],
            halo_send.at[b, 1, piece], halo_recv.at[b, 1, piece],
            device_id={"strip": up}, device_id_type=MESH,
        )

    for b in range(2):
        for piece in range(1):

            @pl.when(has_dn)
            def _():
                to_down(b, piece).start()

            @pl.when(has_up)
            def _():
                to_up(b, piece).start()

    for conv, packed in ((conv_one, k1), (conv_two, k2)):
        packed[...] = jnp.zeros_like(packed)
        flat = jnp.concatenate([conv[i, j] for i in range(3) for j in range(3)], axis=1)
        packed[pl.ds(0, C), pl.ds(0, 9 * C)] = flat
        packed[pl.ds(C, C), :] = jnp.concatenate([jnp.zeros((C, 3 * C), BF), flat], axis=1)
    for b in range(2):
        both = column(noise[pl.ds(b, 1), :], TILE)
        shift[b, pl.ds(0, C), :] = both
        shift[b, pl.ds(C, C), :] = both
    for t in range(BINS):
        ecol[t] = column(embed[pl.ds(t, 1), :], 128)
    gcol[...] = column(gain[...], 128)
    row = lax.broadcasted_iota(jnp.int32, (C, C), 0)
    col = lax.broadcasted_iota(jnp.int32, (C, C), 1)
    perm = jnp.where(col == lax.rem(row, HEADS) * HEAD + row // HEADS, 1.0, 0.0).astype(BF)
    eye = jnp.where(row == col, 1.0, 0.0).astype(BF)
    for index, weight in enumerate((w_key, w_value, w_query)):
        moved = lax.dot_general(
            perm, weight[...], (((1,), (1,)), ((), ())), preferred_element_type=F32
        )
        wqkv[pl.ds(index * C, C), :] = moved.astype(BF)
    moved = jnp.dot(perm, w_out[...], preferred_element_type=F32).astype(BF)
    wout[...] = lax.dot_general(
        eye, moved, (((1,), (1,)), ((), ())), preferred_element_type=F32
    ).astype(BF)
    source = lax.broadcasted_iota(jnp.int32, (TILE, TILE // 2), 0)
    target = lax.broadcasted_iota(jnp.int32, (TILE, TILE // 2), 1)
    table[...] = jnp.where(source // 2 == target, 0.25, 0.0).astype(BF)

    def spread(ref, b, at, value, lo, keep_from):
        width = value.shape[1]
        lane = lax.broadcasted_iota(jnp.int32, (32, width), 1)
        left, right = pltpu.roll(value, 1, 1), pltpu.roll(value, width - 1, 1)
        if lo == 0:
            left = jnp.where(lane == 0, jnp.zeros_like(left), left)
        if lo + width == X:
            right = jnp.where(lane == width - 1, jnp.zeros_like(right), right)
        cols = pl.ds(keep_from, lo + width - keep_from)
        ref[b, pl.ds(at, 32), cols] = left[:, keep_from - lo :]
        ref[b, pl.ds(at + 2 * C, 32), cols] = right[:, keep_from - lo :]

    def activate(b, q0, count, phase=ALL):
        lo, hi, keep_from = phase["act"]

        def body(step, carry):
            q, block = q0 + step // 3, lax.rem(step, 3) * 32
            value = silu(
                xin[b, q, pl.ds(pl.multiple_of(block, 32), 32), pl.ds(lo, hi - lo)].astype(F32)
            ).astype(BF)
            at = pl.multiple_of(q * 288 + block, 32)
            b1[b, pl.ds(at + C, 32), pl.ds(keep_from, hi - keep_from)] = (
                value[:, keep_from - lo :]
            )
            spread(b1, b, at, value, lo, keep_from)
            return carry

        lax.fori_loop(0, 3 * count, body, 0, unroll=6)

    def first_conv(b, pair, phase=ALL):
        lo, hi, keep_from = phase["side"]

        def body(n, carry):
            cols = pl.ds(pl.multiple_of(n * TILE, TILE), TILE)
            start = pl.multiple_of(pair * 576, 64)
            total = jnp.dot(
                k1[...], b1[b, pl.ds(start, 1152), cols], preferred_element_type=F32
            )
            value = silu(total + shift[b])
            off_top = jnp.logical_and(pair == 0, jnp.logical_not(has_up))
            off_end = jnp.logical_and(pair == 2, jnp.logical_not(has_dn))
            upper = jnp.where(off_top, 0.0, value[:C]).astype(BF)
            lower = jnp.where(off_end, 0.0, value[C:]).astype(BF)
            b2[b, pl.ds(pl.multiple_of(start + C, 32), C), cols] = upper
            b2[b, pl.ds(pl.multiple_of(start + 288 + C, 32), C), cols] = lower
            return carry

        lax.fori_loop(*phase["one"], body, 0, unroll=True)

        def sides(step, carry):
            at = pl.multiple_of(pair * 576 + (step // 3) * 288 + lax.rem(step, 3) * 32, 32)
            value = b2[b, pl.ds(at + C, 32), pl.ds(lo, hi - lo)]
            spread(b2, b, at, value, lo, keep_from)
            return carry

        lax.fori_loop(0, 6, sides, 0, unroll=6)

    def second_conv(b, half, phase=ALL):
        def body(n, carry):
            cols = pl.ds(pl.multiple_of(n * TILE, TILE), TILE)
            start = pl.multiple_of(half * 576, 64)
            total = jnp.dot(
                k2[...], b2[b, pl.ds(start, 1152), cols], preferred_element_type=F32
            )
            value = [
                (xin[b, 2 + 2 * half + r, :, cols].astype(F32) + total[r * C : (r + 1) * C]).astype(BF)
                for r in range(2)
            ]
            for r in range(2):
                feat[b, 2 * half + r, :, cols] = value[r]
            mean = jnp.dot(value[0], table[...], preferred_element_type=F32) + jnp.dot(
                value[1], table[...], preferred_element_type=F32
            )
            px = pl.ds(pl.multiple_of(n * (TILE // 2), TILE // 2), TILE // 2)
            pooled[b, half, :, px] = mean.astype(BF)
            pool_far(b, half, px).start()

            @pl.when(half == core)
            def _():
                pool_here(b, half, px).start()

            @pl.when(half != core)
            def _():
                pool_near(b, half, px).start()

            return carry

        lax.fori_loop(*phase["two"], body, 0, unroll=True)

    for b in range(2):
        loads[b].wait()
        activate(b, 2, 4)
        first_conv(b, 1)

    def feature_out(b, half):
        rows = pl.ds(2 * half, 2)
        return pltpu.make_async_copy(feat.at[b, rows], f_ref.at[b, rows], feat_sem.at[b, half])

    def pool_far(b, half, px):
        return pltpu.make_async_remote_copy(
            pooled.at[b, half, :, px], tokens.at[2 * bdev + b, :, px], pool_send.at[b, half, 0],
            pool_recv.at[2 * bdev + b], device_id={"bin": other + half}, device_id_type=MESH,
        )

    def pool_near(b, half, px):
        return pltpu.make_async_remote_copy(
            pooled.at[b, half, :, px], tokens.at[2 * bdev + b, :, px], pool_send.at[b, half, 1],
            pool_recv.at[2 * bdev + b], device_id={"bin": sibling}, device_id_type=MESH,
        )

    def pool_here(b, half, px):
        return pltpu.make_async_copy(
            pooled.at[b, half, :, px], tokens.at[2 * bdev + b, :, px], pool_recv.at[2 * bdev + b]
        )

    whole = pl.ds(0, PX)

    def halo(b, half, pieces):
        @pl.when(half == 0)
        def _():
            for piece in pieces:
                cols = pl.ds(*PIECES[piece])

                @pl.when(has_up)
                def _():
                    to_down(b, piece).wait_recv()

                @pl.when(jnp.logical_not(has_up))
                def _():
                    xin[b, pl.ds(0, 2), :, cols] = jnp.zeros((2, C, PIECES[piece][1]), BF)

        @pl.when(half == 1)
        def _():
            for piece in pieces:
                cols = pl.ds(*PIECES[piece])

                @pl.when(has_dn)
                def _():
                    to_up(b, piece).wait_recv()

                @pl.when(jnp.logical_not(has_dn))
                def _():
                    xin[b, pl.ds(6, 2), :, cols] = jnp.zeros((2, C, PIECES[piece][1]), BF)

    flip = jnp.where(lax.rem(strip, 4) == 0, 1, 0)

    def units(b, pieces, phase, final):
        def unit(step, carry):
            half = lax.rem(step + flip, 2)
            halo(b, half, pieces)
            activate(b, 6 * half, 2, phase)
            first_conv(b, 2 * half, phase)
            second_conv(b, half, phase)
            if final:
                feature_out(b, half).start()
            return carry

        lax.fori_loop(0, 2, unit, 0)

    units(0, (0,), ALL, True)
    units(1, (0,), ALL, True)

    def token(t):
        return [
            tokens[t, :, pl.ds(n * 128, 128)].astype(F32) + ecol[t] for n in range(PX // 128)
        ]

    def project(step, carry):
        step_dev = lax.rem(step, 4)
        peer = 2 * lax.rem(xh + step_dev // 2, 2) + lax.rem(core + step_dev, 2)
        t = 2 * peer + step // 4
        pltpu.make_async_copy(tokens.at[t], tokens.at[t], pool_recv.at[t]).wait()
        normed = []
        for z in token(t):
            center = jnp.sum(z, axis=0, keepdims=True) * (1.0 / C)
            delta = z - center
            spread_of = jnp.sum(delta * delta, axis=0, keepdims=True) * (1.0 / C)
            normed.append((delta * lax.rsqrt(spread_of + 1e-05) * gcol[...]).astype(BF))
        qkv[t] = jnp.dot(
            wqkv[...], jnp.concatenate(normed, axis=1), preferred_element_type=F32
        )
        return carry

    lax.fori_loop(0, BINS, project, 0, unroll=4)

    scale = 1.0 / (HEAD**0.5)

    def back(b, px):
        return pltpu.make_async_remote_copy(
            result.at[2 * (1 - core) + b, :, px], o_ref.at[b, core, :, px], back_send.at[b],
            back_recv.at[b], device_id={"bin": sibling}, device_id_type=MESH,
        )

    def keep(b, px):
        return pltpu.make_async_copy(
            result.at[2 * core + b, :, px], o_ref.at[b, core, :, px], load_sem.at[b]
        )

    def attend(n, carry):
        px = pl.ds(pl.multiple_of(n * 128, 128), 128)

        def one(index, carry):
            t = xh * 4 + index
            query = (qkv[t, pl.ds(2 * C, C), px] * scale).reshape(12, 8, 128)
            numer = jnp.zeros((12, 8, 128), F32)
            denom = jnp.zeros((8, 128), F32)
            for u in range(BINS):
                score = jnp.sum(query * qkv[u, pl.ds(0, C), px].reshape(12, 8, 128), axis=0)
                expo = jnp.exp(score + pltpu.roll(score, 4, 0))
                denom = denom + expo
                numer = numer + qkv[u, pl.ds(C, C), px].reshape(12, 8, 128) * expo[None]
            mixed[:, pl.ds(pl.multiple_of(index * 128, 128), 128)] = (
                (numer / denom[None]).reshape(C, 128).astype(BF)
            )
            return carry

        lax.fori_loop(0, 4, one, 0, unroll=2)
        delta = jnp.dot(wout[...], mixed[...], preferred_element_type=F32)
        for index in range(4):
            t = xh * 4 + index
            result[index, :, px] = (
                tokens[t, :, px].astype(F32) + ecol[t] + delta[:, index * 128 : (index + 1) * 128]
            ).astype(BF)
        for b in range(2):
            back(b, px).start()
            keep(b, px).start()
        return carry

    lax.fori_loop(0, PX // 128, attend, 0)

    def drain(step, carry):
        b, half = step // 2, lax.rem(step, 2)
        feature_out(b, half).wait()
        pool_far(b, half, whole).wait_send()

        @pl.when(half != core)
        def _():
            pool_near(b, half, whole).wait_send()

        return carry

    lax.fori_loop(0, 4, drain, 0)
    for b in range(2):

        for piece in range(1):

            @pl.when(has_dn)
            def _():
                to_down(b, piece).wait_send()

            @pl.when(has_up)
            def _():
                to_up(b, piece).wait_send()

        back(b, whole).wait()
        keep(b, whole).wait()


def local(
    maps_in, conv_one, conv_two, noise_shift, bin_embed, norm_gain, w_query, w_key, w_value, w_out
):
    whole = pl.BlockSpec(memory_space=pltpu.VMEM)
    hbm = pl.BlockSpec(memory_space=pl.ANY)
    return pl.pallas_call(
        kernel,
        out_shape=(
            jax.ShapeDtypeStruct((2, 4, C, X), BF),
            jax.ShapeDtypeStruct((2, 2, C, PX), BF),
        ),
        in_specs=[hbm] + [whole] * 9,
        out_specs=(hbm, hbm),
        scratch_shapes=[
            pltpu.VMEM((2, 8, C, X), BF),
            pltpu.VMEM((2 * C, 12 * C), BF),
            pltpu.VMEM((2 * C, 12 * C), BF),
            pltpu.VMEM((2, 24 * C, X), BF),
            pltpu.VMEM((2, 18 * C, X), BF),
            pltpu.VMEM((2, 4, C, X), BF),
            pltpu.VMEM((2, 2 * C, TILE), F32),
            pltpu.VMEM((BINS, C, 128), F32),
            pltpu.VMEM((C, 128), F32),
            pltpu.VMEM((3 * C, C), BF),
            pltpu.VMEM((C, C), BF),
            pltpu.VMEM((TILE, TILE // 2), BF),
            pltpu.VMEM((2, 2, C, PX), BF),
            pltpu.VMEM((BINS, C, PX), BF),
            pltpu.VMEM((BINS, 3 * C, PX), F32),
            pltpu.VMEM((C, PX), BF),
            pltpu.VMEM((4, C, PX), BF),
            pltpu.SemaphoreType.DMA((2,)),
            pltpu.SemaphoreType.DMA((2, 2, 2)),
            pltpu.SemaphoreType.DMA((2, 2, 2)),
            pltpu.SemaphoreType.DMA((2, 2)),
            pltpu.SemaphoreType.DMA((2, 2, 2)),
            pltpu.SemaphoreType.DMA((BINS,)),
            pltpu.SemaphoreType.DMA((2,)),
            pltpu.SemaphoreType.DMA((2,)),
        ],
        compiler_params=pltpu.CompilerParams(
            collective_id=0, has_side_effects=True, vmem_limit_bytes=60 * 1024 * 1024
        ),
        name="resblock_attention",
    )(
        maps_in, conv_one, conv_two, noise_shift, bin_embed, norm_gain.reshape(1, C),
        w_query, w_key, w_value, w_out,
    )


def solution(mesh):
    in_specs = (
        P("bin", "strip", None, None),
        P(),
        P(),
        P("bin", None),
        P(),
        P(),
        P(),
        P(),
        P(),
        P(),
    )
    out_specs = (P("bin", "strip", None, None), P("bin", "strip", None, None))
    return jax.shard_map(local, mesh=mesh, in_specs=in_specs, out_specs=out_specs, check_vma=False)
```
